768 devices in a mesh: role: 4 (over y_hi), band: 24 (over y_lo, z), turn: 8 (over x, core).
Axes of the slice: x: 4, y: 8 (y_hi: 4, y_lo: 2; y = y_hi * 2 + y_lo), z: 12, core: 2. Of those that a mesh axis runs over, the one named last changes fastest.
Arguments:
- voltages: bfloat16 [96, 2, 256, 3840], P(('role', 'band'), None, 'turn'), may hold values from -6 to 6
- station_flags: int32 [256], P('turn'), may hold values 0 or 1
- filter_taps: bfloat16 [8, 256, 256], replicated, may hold values from -0.125 to 0.125
- kernel_rows: bfloat16 [96, 1, 32, 256], P(('role', 'band')), may hold values from -0.375 to 0.375
- kernel_cols: bfloat16 [96, 1, 32, 256], P(('role', 'band')), may hold values from -0.375 to 0.375
- cell_index: int32 [2, 12288, 1], P(None, ('role', 'band', 'turn')), may hold values from 0 to 4095
Outputs:
- image: float32 [768, 128], P(('role', 'band', 'turn'))
The draws below stay inside these ranges and needn't reach their ends.
All inputs are finite; a program needn't handle non-finite values. No bound on the sum of `station_flags` on one device may be relied on, other than what follows from the above.
Results may differ from the reference program's by a relative error of at most 0.0071.
Values may be sent and summed in bfloat16 or wider, within the bound.
A program may use at most 32 MiB of HBM per device.

```python
import math
import jax
import jax.numpy as jnp
from jax import lax

STATIONS = 256
FINE = 128
TAPS = 8
FRAMES = 8
BLK = 256
SU = 32
SV = 32
NGRID = 4096
MW = 128
COARSE = 96
CHANNELS = 12288
NBLK = 1
LW = 768


def touch_ends(values, rng, smallest, top_value):
    index_at = [jax.random.randint(jax.random.fold_in(rng, axis), (), 0, length) for axis, length in enumerate(values.shape)]
    widest = values.shape.index(max(values.shape))
    neighbour = index_at[:widest] + [(index_at[widest] + 1) % values.shape[widest]] + index_at[widest + 1:]
    return values.at[tuple(index_at)].set(smallest).at[tuple(neighbour)].set(top_value)


def level_of(own_key, dims, split, low, largest):
    level = 1.0
    for dim, parts in split:
        heights = jax.random.uniform(jax.random.fold_in(jax.random.fold_in(own_key, 6), dim), (parts,), jnp.float32, low / len(split), largest / len(split))
        level = level * jnp.repeat(jnp.exp(heights), dims[dim] // parts).reshape((-1,) + (1,) * (len(dims) - 1 - dim))
    return level


def noise(own_key, extent, width, most, split=(), held_as=jnp.bfloat16):
    values = jax.random.normal(own_key, extent, jnp.float32) * width
    if len(split) > 0:
        values = level_of(own_key, extent, split, -0.22, 0.18) * values
    return jnp.clip(values, min=-most, max=most).astype(held_as)


def setup_inputs(seed: int = 0) -> dict:
    streams_of = jax.random.split(jax.random.key(seed), 7)
    voltages = noise(streams_of[0], (COARSE, 2, STATIONS, (FRAMES + TAPS - 1) * 2 * FINE), 1.0, 6.0, ((0, 96), (2, 8)))
    station_flags = touch_ends((jax.random.randint(streams_of[1], (STATIONS,), 0, 8) < 7).astype(jnp.int32), jax.random.fold_in(streams_of[1], 1), 0, 1)
    filter_taps = noise(streams_of[2], (TAPS, 2 * FINE, 2 * FINE), (TAPS * 2 * FINE) ** -0.5, 0.125)
    kernel_rows = noise(streams_of[3], (COARSE, NBLK, SU, BLK), BLK ** -0.5, 0.375, ((0, 96),))
    kernel_cols = noise(streams_of[4], (COARSE, NBLK, SV, BLK), BLK ** -0.5, 0.375, ((0, 96),))
    cell_index = touch_ends(jax.random.randint(streams_of[5], (2, CHANNELS, NBLK * NBLK), 0, NGRID), jax.random.fold_in(streams_of[5], 1), 0, NGRID - 1).astype(jnp.int32)
    return {"voltages": voltages, "station_flags": station_flags, "filter_taps": filter_taps, "kernel_rows": kernel_rows, "kernel_cols": kernel_cols, "cell_index": cell_index}


HIGHEST = lax.Precision.HIGHEST

def channelize(voltages, station_flags, filter_taps):
    polars, station_rows, sample_width = voltages.shape
    tap_count, two_fine, _ = filter_taps.shape
    block_total = sample_width // two_fine
    frames = block_total - tap_count + 1
    flagged = voltages * station_flags[None, :, None].astype(voltages.dtype)
    blocks = flagged.reshape(polars * station_rows, block_total, two_fine)
    running = jnp.zeros((polars * station_rows * frames, two_fine), jnp.float32)
    for tap_index in range(tap_count):
        segment = blocks[:, tap_index:tap_index + frames, :].reshape(polars * station_rows * frames, two_fine)
        running = running + jnp.dot(segment, filter_taps[tap_index], preferred_element_type=jnp.float32)
    fine_count = two_fine // 2
    result = running.astype(jnp.bfloat16).reshape(polars, station_rows, frames, 2, fine_count)
    return jnp.transpose(result, (4, 0, 1, 3, 2)).reshape(fine_count, polars, station_rows, 2 * frames)

def correlate(spectra):
    frames = spectra.shape[3] // 2
    station_count = spectra.shape[2]
    swapped = jnp.concatenate([-spectra[..., frames:], spectra[..., :frames]], axis=3)
    stacked = jnp.concatenate([spectra, swapped], axis=2)
    products = jnp.einsum('fpsa,fpka->fpsk', spectra.astype(jnp.float32), stacked.astype(jnp.float32), precision=HIGHEST)
    stokes = (products[:, 0] + products[:, 1]) * (1.0 / frames)
    return jnp.stack([stokes[:, :, :station_count], stokes[:, :, station_count:]]).astype(jnp.bfloat16)

def subgrids(visibility, kernel_rows, kernel_cols):
    fine_local = visibility.shape[1]
    station_count = visibility.shape[2]
    block_count, sub_u, block_width = kernel_rows.shape
    sub_v = kernel_cols.shape[1]
    station_rows = visibility.reshape(2, fine_local, block_count, block_width, station_count)
    partial_value = jnp.einsum('iab,xfibs->xfias', kernel_rows.astype(jnp.float32), station_rows.astype(jnp.float32), precision=HIGHEST)
    partial_value = partial_value.reshape(2, fine_local, block_count, sub_u, block_count, block_width)
    result = jnp.einsum('xfiajc,jdc->xfijad', partial_value, kernel_cols.astype(jnp.float32), precision=HIGHEST)
    return result.reshape(2, fine_local, block_count * block_count, sub_u * sub_v).astype(jnp.bfloat16)

def fine_subgrids(spectra, kernel_rows, kernel_cols):

    def one_fine(spec_one):
        return subgrids(correlate(spec_one[None]), kernel_rows, kernel_cols)[:, 0]
    stacked = lax.map(one_fine, spectra)
    return jnp.transpose(stacked, (1, 0, 2, 3))

def phase_table(positions, offset_count, pixels, grid_size):
    offsets = jnp.arange(offset_count, dtype=jnp.int32)
    position = positions[:, None, None].astype(jnp.int32) + offsets[None, :, None]
    phase_turns = jnp.mod(position * pixels[None, None, :], grid_size)
    angles = phase_turns.astype(jnp.float32) * (2.0 * math.pi / grid_size)
    return (jnp.cos(angles).astype(jnp.bfloat16), jnp.sin(angles).astype(jnp.bfloat16))

def image_rows(subgrid, positions, row_first, row_count, row_total, sub_u, sub_v, col_total, grid_size):
    count_sub = subgrid.shape[1]
    row_pix = row_first + jnp.arange(row_count, dtype=jnp.int32) - row_total // 2
    col_pix = jnp.arange(col_total, dtype=jnp.int32) - col_total // 2
    row_cos, row_sin = phase_table(positions[0], sub_u, row_pix, grid_size)
    col_cos, col_sin = phase_table(positions[1], sub_v, col_pix, grid_size)
    sub_cells = subgrid.reshape(2, count_sub, sub_u, sub_v).astype(jnp.float32)
    row_cos = row_cos.astype(jnp.float32)
    row_sin = row_sin.astype(jnp.float32)
    proj_real = (jnp.einsum('nal,nab->nbl', row_cos, sub_cells[0], precision=HIGHEST) - jnp.einsum('nal,nab->nbl', row_sin, sub_cells[1], precision=HIGHEST)).astype(jnp.bfloat16)
    proj_imag = (jnp.einsum('nal,nab->nbl', row_cos, sub_cells[1], precision=HIGHEST) + jnp.einsum('nal,nab->nbl', row_sin, sub_cells[0], precision=HIGHEST)).astype(jnp.bfloat16)
    return jnp.einsum('nbl,nbm->lm', proj_real.astype(jnp.float32), col_cos.astype(jnp.float32), precision=HIGHEST) - jnp.einsum('nbl,nbm->lm', proj_imag.astype(jnp.float32), col_sin.astype(jnp.float32), precision=HIGHEST)

def reference(voltages, station_flags, filter_taps, kernel_rows, kernel_cols, cell_index):
    positions_all = jnp.transpose(cell_index.reshape(2, COARSE, FINE * NBLK * NBLK), (1, 0, 2))

    def per_coarse(running, inputs_now):
        volt_now, rows_now, cols_now, places_now = inputs_now
        spectra = channelize(volt_now, station_flags, filter_taps)
        subgrid = fine_subgrids(spectra, rows_now, cols_now).reshape(2, FINE * NBLK * NBLK, SU * SV)
        return (running + image_rows(subgrid, places_now, 0, LW, LW, SU, SV, MW, NGRID), None)
    running, _ = lax.scan(per_coarse, jnp.zeros((LW, MW), jnp.float32), (voltages, kernel_rows, kernel_cols, positions_all))
    scale_factor = 4.0 / math.sqrt(CHANNELS * NBLK * NBLK * SU * SV)
    return running * scale_factor
```

```python
import math

import jax
import jax.numpy as jnp
from jax import lax
from jax.experimental import pallas as pl
from jax.experimental.pallas import tpu as pltpu
from jax.sharding import PartitionSpec as P

MESH = pl.DeviceIdType.MESH
F32 = jnp.float32
BF16 = jnp.bfloat16
I32 = jnp.int32

NGRID = 4096
NT, NY, NZ = 8, 8, 12
FINE = 128
FLOC = 16
STLOC = 32
TAPS = 8
FRAMES = 8
SUB = 32
MW = 128
LW = NT * NY * NZ
PIECE = NY * NZ
SCALE = 4.0 / math.sqrt(96 * FINE * SUB * SUB)
CHUNK = 256


def iota(shape, dim):
    return lax.broadcasted_iota(I32, shape, dim)


def trig(turns):
    shifted = turns + 512
    quadrant = shifted >> 10
    x = ((shifted & 1023) - 512).astype(F32) * (2.0 * math.pi / NGRID)
    x2 = x * x
    s = x * (1.0 + x2 * (-1.0 / 6 + x2 * (1.0 / 120 + x2 * (-1.0 / 5040 + x2 * (1.0 / 362880)))))
    c = 1.0 + x2 * (-0.5 + x2 * (1.0 / 24 + x2 * (-1.0 / 720 + x2 * (1.0 / 40320))))
    odd = (quadrant & 1) == 1
    cos = jnp.where(odd, s, c)
    sin = jnp.where(odd, c, s)
    cos = jnp.where(((quadrant + 1) & 2) == 2, -cos, cos)
    sin = jnp.where((quadrant & 2) == 2, -sin, sin)
    return cos, sin


def split(x):
    high = x.astype(BF16)
    return high, (x - high.astype(F32)).astype(BF16)


def channelize(v_ref, flag_ref, taps_ref, xs_ref):
    width = 2 * FINE
    lhs = jnp.concatenate(
        [v_ref[:, t * width : (t + TAPS) * width] for t in range(FRAMES)], axis=0
    )
    out = jnp.dot(lhs, taps_ref[...], preferred_element_type=F32)
    lane = iota((1, 128), 1) & (STLOC - 1)
    flags = jnp.zeros((1, 128), F32)
    for s in range(STLOC):
        flags = jnp.where(lane == s, flag_ref[s].astype(F32), flags)
    turned = (out.T * jnp.concatenate([flags] * 4, axis=1)).astype(BF16)
    for d in range(NT):
        for c in range(2):
            xs_ref[d, c] = turned[c * FINE + d * FLOC : c * FINE + (d + 1) * FLOC, :]


def tables(mt, my, mz, cell_ref, t0_ref, ph_ref, ct_ref):
    lane = iota((1, LW), 1)
    kt = jnp.zeros((1, LW), I32)
    for i in range(1, NT):
        kt = kt + (lane >= PIECE * i).astype(I32)
    j = lane - PIECE * kt
    z = mz + 1 + (j >> 3)
    z = jnp.where(z >= NZ, z - NZ, z)
    y = (my + 1 + (j & 7)) & (NY - 1)
    t = (mt + 1 + kt) & (NT - 1)
    pix = NT * (NZ * y + z) + t - LW // 2
    cos, sin = trig(iota((SUB, LW), 0) * pix)
    cos_hi, cos_lo = split(cos)
    sin_hi, sin_lo = split(sin)
    t0_ref[0:32] = cos_hi
    t0_ref[32:64] = sin_hi
    t0_ref[64:96] = cos_lo
    t0_ref[96:128] = sin_lo
    row = iota((FLOC, LW), 0)
    cell_u = jnp.zeros((FLOC, LW), I32)
    for n in range(FLOC):
        cell_u = jnp.where(row == n, cell_ref[0, n], cell_u)
    cos, sin = trig(cell_u * pix)
    ph_ref[0] = cos
    ph_ref[1] = sin
    lane = iota((1, FLOC * SUB), 1)
    cell_v = jnp.zeros((1, FLOC * SUB), I32)
    for n in range(FLOC):
        cell_v = jnp.where((lane >> 5) == n, cell_ref[1, n], cell_v)
    cell_v = cell_v + (lane & 31)
    cos, sin = trig((iota((MW, FLOC * SUB), 0) - MW // 2) * cell_v)
    ct_ref[:, : FLOC * SUB] = cos.astype(BF16)
    ct_ref[:, FLOC * SUB :] = (-sin).astype(BF16)


def weights(kr_ref, kc_ref, w_ref):
    w_ref[...] = jnp.zeros(w_ref.shape, BF16)
    for side, k_ref in enumerate((kr_ref, kc_ref)):
        k = k_ref[...].astype(F32)
        kt = jnp.concatenate([k] * 4, axis=0).T.astype(BF16)
        for src in range(NT):
            for q in range(4):
                w_ref[
                    src * 128 + q * 32 : src * 128 + (q + 1) * 32,
                    side * 512 + q * 128 : side * 512 + (q + 1) * 128,
                ] = kt[src * 32 : (src + 1) * 32, :]


def subgrids(xr_ref, w_ref, ab_ref, sall_ref):
    lhs = jnp.concatenate(
        [
            jnp.concatenate([xr_ref[src, c, :, g * 128 : (g + 1) * 128] for src in range(NT)], axis=1)
            for g in range(4)
            for c in range(2)
        ],
        axis=0,
    )
    out = jnp.dot(lhs, w_ref[...], preferred_element_type=F32)
    u = out[:, :512]
    v = jnp.concatenate(
        [
            u[(2 * g + 1) * FLOC : (2 * g + 2) * FLOC] if c == 0 else -u[2 * g * FLOC : (2 * g + 1) * FLOC]
            for g in range(4)
            for c in range(2)
        ],
        axis=0,
    )
    odd = ((iota((128, 512), 1) >> 5) & 1) == 1
    real = jnp.where(odd, -v, u)
    imag = jnp.where(odd, u, v)
    for q in range(4):
        part = slice(q * 128, (q + 1) * 128)
        ab_ref[0, q] = real[:, part]
        ab_ref[1, q] = imag[:, part]
        ab_ref[2, q] = out[:, 512 + q * 128 : 512 + (q + 1) * 128]
    same = (iota((128, 128), 0) >> 5) == (iota((128, 128), 1) >> 5)
    for h in range(4):

        def gather(k):
            return jnp.concatenate(
                [
                    ab_ref[k, q, pl.ds(fl, 8, stride=FLOC), :]
                    for fl in range(4 * h, 4 * h + 4)
                    for q in range(4)
                ],
                axis=0,
            )

        b_hi, b_lo = split(jnp.where(same, gather(2), 0.0).T)
        a_hi, a_lo = split(jnp.concatenate([gather(0), gather(1)], axis=1))
        sub = (
            jnp.dot(b_hi, a_hi, preferred_element_type=F32)
            + jnp.dot(b_lo, a_hi, preferred_element_type=F32)
            + jnp.dot(b_hi, a_lo, preferred_element_type=F32)
        ) * (1.0 / FRAMES)
        sub = sub.astype(BF16)
        sall_ref[0, h * 128 : (h + 1) * 128, :] = sub[:, :128]
        sall_ref[1, h * 128 : (h + 1) * 128, :] = sub[:, 128:]


def image_chunk(chunk, sall_ref, t0_ref, ph_ref, ct_ref):
    part = slice(chunk * CHUNK, (chunk + 1) * CHUNK)
    table = t0_ref[:, part]
    g_r = jnp.dot(sall_ref[0], table, preferred_element_type=F32).reshape(FLOC, SUB, CHUNK)
    g_i = jnp.dot(sall_ref[1], table, preferred_element_type=F32).reshape(FLOC, SUB, CHUNK)
    cos = ph_ref[0, :, part][:, None, :]
    sin = ph_ref[1, :, part][:, None, :]
    p_r = (cos * g_r - sin * g_i).astype(BF16).reshape(FLOC * SUB, CHUNK)
    p_i = (cos * g_i + sin * g_r).astype(BF16).reshape(FLOC * SUB, CHUNK)
    image = jnp.dot(ct_ref[...], jnp.concatenate([p_r, p_i], axis=0), preferred_element_type=F32)
    return image.T


def kernel(
    v_ref, flag_ref, taps_ref, kr_ref, kc_ref, cell_ref, out_ref,
    xs_ref, xr_ref, t0_ref, ph_ref, ct_ref, w_ref, ab_ref, sall_ref, img_ref,
    tr_ref, zs_ref, zr_ref, ys_ref, yr_ref,
    own_sem, a_send, a_recv, t_send, t_recv, z_send, z_recv, y_send, y_recv,
):
    role = lax.axis_index("role")
    band = lax.axis_index("band")
    mt = lax.axis_index("turn")
    y_lo = band // NZ
    mz = band % NZ
    my = 2 * role + y_lo

    def turn_of(k):
        return {"turn": (mt + 1 + k) % NT}

    def z_of(k):
        return {"band": y_lo * NZ + (mz + 1 + k) % NZ}

    def y_of(k):
        y = (my + 1 + k) % NY
        return {"role": y // 2, "band": (y % 2) * NZ + mz}

    barrier = pltpu.get_barrier_semaphore()
    for k in range(NT - 1):
        pl.semaphore_signal(barrier, inc=1, device_id=turn_of(k), device_id_type=MESH)
    for k in range(NZ - 1):
        pl.semaphore_signal(barrier, inc=1, device_id=z_of(k), device_id_type=MESH)
    for k in range(NY - 1):
        pl.semaphore_signal(barrier, inc=1, device_id=y_of(k), device_id_type=MESH)

    channelize(v_ref, flag_ref, taps_ref, xs_ref)

    pl.semaphore_wait(barrier, NT + NZ + NY - 3)
    spread = []
    for k in range(NT - 1):
        dest = (mt + 1 + k) % NT
        copy = pltpu.make_async_remote_copy(
            src_ref=xs_ref.at[dest], dst_ref=xr_ref.at[mt],
            send_sem=a_send.at[k], recv_sem=a_recv.at[mt],
            device_id=turn_of(k), device_id_type=MESH,
        )
        copy.start()
        spread.append(copy)
    own = pltpu.make_async_copy(xs_ref.at[mt], xr_ref.at[mt], own_sem)
    own.start()

    tables(mt, my, mz, cell_ref, t0_ref, ph_ref, ct_ref)
    weights(kr_ref, kc_ref, w_ref)

    own.wait()
    for k in range(NT - 1):
        src = (mt + 1 + k) % NT
        pltpu.make_async_remote_copy(
            src_ref=xs_ref.at[src], dst_ref=xr_ref.at[src],
            send_sem=a_send.at[k], recv_sem=a_recv.at[src],
            device_id=turn_of(k), device_id_type=MESH,
        ).wait_recv()

    subgrids(xr_ref, w_ref, ab_ref, sall_ref)

    def turn_copy(k):
        return pltpu.make_async_remote_copy(
            src_ref=img_ref.at[pl.ds(k * PIECE, PIECE), :], dst_ref=tr_ref.at[k],
            send_sem=t_send.at[k], recv_sem=t_recv.at[k],
            device_id=turn_of(k), device_id_type=MESH,
        )

    turn_copies = []
    done = 0
    for chunk in range(LW // CHUNK):
        rows = image_chunk(chunk, sall_ref, t0_ref, ph_ref, ct_ref)
        img_ref[chunk * CHUNK : (chunk + 1) * CHUNK, :] = rows.astype(BF16)
        while done < NT - 1 and (done + 1) * PIECE <= (chunk + 1) * CHUNK:
            copy = turn_copy(done)
            copy.start()
            turn_copies.append(copy)
            done += 1
    total = rows[CHUNK - PIECE :, :]
    for k in range(NT - 1):
        turn_copies[k].wait_recv()
        total = total + tr_ref[k].astype(F32)

    zs_ref[...] = total.reshape(NZ, NY, MW)
    z_copies = []
    for k in range(NZ - 1):
        copy = pltpu.make_async_remote_copy(
            src_ref=zs_ref.at[k], dst_ref=zr_ref.at[k],
            send_sem=z_send.at[k], recv_sem=z_recv.at[k],
            device_id=z_of(k), device_id_type=MESH,
        )
        copy.start()
        z_copies.append(copy)
    total = total[(NZ - 1) * NY :, :]
    for k in range(NZ - 1):
        z_copies[k].wait_recv()
        total = total + zr_ref[k]

    y_copies = []
    for k in range(NY):
        ys_ref[k] = total[k : k + 1, :]
    for k in range(NY - 1):
        copy = pltpu.make_async_remote_copy(
            src_ref=ys_ref.at[k], dst_ref=yr_ref.at[k],
            send_sem=y_send.at[k], recv_sem=y_recv.at[k],
            device_id=y_of(k), device_id_type=MESH,
        )
        copy.start()
        y_copies.append(copy)
    final = total[NY - 1 : NY, :]
    for k in range(NY - 1):
        y_copies[k].wait_recv()
        final = final + yr_ref[k]
    out_ref[...] = final * SCALE
    for copy in spread + turn_copies + z_copies + y_copies:
        copy.wait_send()


def local(voltages, station_flags, filter_taps, kernel_rows, kernel_cols, cell_index):
    vmem = pl.BlockSpec(memory_space=pltpu.VMEM)
    smem = pl.BlockSpec(memory_space=pltpu.SMEM)
    dma = pltpu.SemaphoreType.DMA
    return pl.pallas_call(
        kernel,
        out_shape=jax.ShapeDtypeStruct((1, MW), F32),
        in_specs=[vmem, smem, vmem, vmem, vmem, smem],
        out_specs=vmem,
        scratch_shapes=[
            pltpu.VMEM((NT, 2, FLOC, 512), BF16),
            pltpu.VMEM((NT, 2, FLOC, 512), BF16),
            pltpu.VMEM((128, LW), BF16),
            pltpu.VMEM((2, FLOC, LW), F32),
            pltpu.VMEM((MW, 2 * FLOC * SUB), BF16),
            pltpu.VMEM((1024, 1024), BF16),
            pltpu.VMEM((3, 4, 128, 128), F32),
            pltpu.VMEM((2, FLOC * SUB, 128), BF16),
            pltpu.VMEM((LW, MW), BF16),
            pltpu.VMEM((NT - 1, PIECE, MW), BF16),
            pltpu.VMEM((NZ, NY, MW), F32),
            pltpu.VMEM((NZ - 1, NY, MW), F32),
            pltpu.VMEM((NY, 1, MW), F32),
            pltpu.VMEM((NY - 1, 1, MW), F32),
            dma,
            dma((NT - 1,)),
            dma((NT,)),
            dma((NT - 1,)),
            dma((NT - 1,)),
            dma((NZ - 1,)),
            dma((NZ - 1,)),
            dma((NY - 1,)),
            dma((NY - 1,)),
        ],
        compiler_params=pltpu.CompilerParams(collective_id=0, has_side_effects=True),
    )(
        voltages.reshape(2 * STLOC, -1),
        station_flags,
        filter_taps.reshape(TAPS * 2 * FINE, 2 * FINE),
        kernel_rows.reshape(SUB, -1),
        kernel_cols.reshape(SUB, -1),
        cell_index.reshape(2, FLOC),
    )


def solution(mesh):
    in_specs = (
        P(("role", "band"), None, "turn", None),
        P("turn"),
        P(),
        P(("role", "band"), None, None, None),
        P(("role", "band"), None, None, None),
        P(None, ("role", "band", "turn"), None),
    )
    out_specs = P(("role", "band", "turn"), None)
    return jax.shard_map(local, mesh=mesh, in_specs=in_specs, out_specs=out_specs, check_vma=False)
```

```python
import math

import jax
import jax.numpy as jnp
from jax import lax
from jax.experimental import pallas as pl
from jax.experimental.pallas import tpu as pltpu
from jax.sharding import PartitionSpec as P

MESH = pl.DeviceIdType.MESH
F32 = jnp.float32
BF16 = jnp.bfloat16
I32 = jnp.int32

NGRID = 4096
NT, NY, NZ = 8, 8, 12
FINE = 128
FLOC = 16
STLOC = 32
TAPS = 8
FRAMES = 8
SUB = 32
MW = 128
LW = NT * NY * NZ
PIECE = NY * NZ
SCALE = 4.0 / math.sqrt(96 * FINE * SUB * SUB)
CHUNK = 256


def iota(shape, dim):
    return lax.broadcasted_iota(I32, shape, dim)


def trig(turns):
    shifted = turns + 512
    quadrant = shifted >> 10
    x = ((shifted & 1023) - 512).astype(F32) * (2.0 * math.pi / NGRID)
    x2 = x * x
    s = x * (1.0 + x2 * (-1.0 / 6 + x2 * (1.0 / 120 + x2 * (-1.0 / 5040 + x2 * (1.0 / 362880)))))
    c = 1.0 + x2 * (-0.5 + x2 * (1.0 / 24 + x2 * (-1.0 / 720 + x2 * (1.0 / 40320))))
    odd = (quadrant & 1) == 1
    cos = jnp.where(odd, s, c)
    sin = jnp.where(odd, c, s)
    cos = jnp.where(((quadrant + 1) & 2) == 2, -cos, cos)
    sin = jnp.where((quadrant & 2) == 2, -sin, sin)
    return cos, sin


def split(x):
    high = x.astype(BF16)
    return high, (x - high.astype(F32)).astype(BF16)


def channelize(v_ref, flag_ref, taps_ref, xs_ref):
    width = 2 * FINE
    lhs = jnp.concatenate(
        [v_ref[:, t * width : (t + TAPS) * width] for t in range(FRAMES)], axis=0
    )
    out = jnp.dot(lhs, taps_ref[...], preferred_element_type=F32)
    lane = iota((1, 128), 1) & (STLOC - 1)
    flags = jnp.zeros((1, 128), F32)
    for s in range(STLOC):
        flags = jnp.where(lane == s, flag_ref[s].astype(F32), flags)
    turned = (out.T * jnp.concatenate([flags] * 4, axis=1)).astype(BF16)
    for d in range(NT):
        for c in range(2):
            xs_ref[d, c] = turned[c * FINE + d * FLOC : c * FINE + (d + 1) * FLOC, :]


def tables(mt, my, mz, cell_ref, t0_ref, ph_ref, ct_ref):
    lane = iota((1, LW), 1)
    kt = jnp.zeros((1, LW), I32)
    for i in range(1, NT):
        kt = kt + (lane >= PIECE * i).astype(I32)
    j = lane - PIECE * kt
    z = mz + 1 + (j >> 3)
    z = jnp.where(z >= NZ, z - NZ, z)
    y = (my + 1 + (j & 7)) & (NY - 1)
    t = (mt + 1 + kt) & (NT - 1)
    pix = NT * (NZ * y + z) + t - LW // 2
    cos, sin = trig(iota((SUB, LW), 0) * pix)
    cos_hi, cos_lo = split(cos)
    sin_hi, sin_lo = split(sin)
    t0_ref[0:32] = cos_hi
    t0_ref[32:64] = sin_hi
    t0_ref[64:96] = cos_lo
    t0_ref[96:128] = sin_lo
    row = iota((FLOC, LW), 0)
    cell_u = jnp.zeros((FLOC, LW), I32)
    for n in range(FLOC):
        cell_u = jnp.where(row == n, cell_ref[0, n], cell_u)
    cos, sin = trig(cell_u * pix)
    ph_ref[0] = cos
    ph_ref[1] = sin
    lane = iota((1, FLOC * SUB), 1)
    cell_v = jnp.zeros((1, FLOC * SUB), I32)
    for n in range(FLOC):
        cell_v = jnp.where((lane >> 5) == n, cell_ref[1, n], cell_v)
    cell_v = cell_v + (lane & 31)
    cos, sin = trig((iota((MW, FLOC * SUB), 0) - MW // 2) * cell_v)
    ct_ref[:, : FLOC * SUB] = cos.astype(BF16)
    ct_ref[:, FLOC * SUB :] = (-sin).astype(BF16)


def weights(kr_ref, kc_ref, w_ref):
    w_ref[...] = jnp.zeros(w_ref.shape, BF16)
    for side, k_ref in enumerate((kr_ref, kc_ref)):
        k = k_ref[...].astype(F32)
        kt = jnp.concatenate([k] * 4, axis=0).T.astype(BF16)
        for src in range(NT):
            for q in range(4):
                w_ref[
                    src * 128 + q * 32 : src * 128 + (q + 1) * 32,
                    side * 512 + q * 128 : side * 512 + (q + 1) * 128,
                ] = kt[src * 32 : (src + 1) * 32, :]


def subgrids(xr_ref, w_ref, ab_ref, sall_ref):
    lhs = jnp.concatenate(
        [
            jnp.concatenate([xr_ref[src, c, :, g * 128 : (g + 1) * 128] for src in range(NT)], axis=1)
            for g in range(4)
            for c in range(2)
        ],
        axis=0,
    )
    out = jnp.dot(lhs, w_ref[...], preferred_element_type=F32)
    u = out[:, :512]
    v = jnp.concatenate(
        [
            u[(2 * g + 1) * FLOC : (2 * g + 2) * FLOC] if c == 0 else -u[2 * g * FLOC : (2 * g + 1) * FLOC]
            for g in range(4)
            for c in range(2)
        ],
        axis=0,
    )
    odd = ((iota((128, 512), 1) >> 5) & 1) == 1
    real = jnp.where(odd, -v, u)
    imag = jnp.where(odd, u, v)
    for q in range(4):
        part = slice(q * 128, (q + 1) * 128)
        ab_ref[0, q] = real[:, part]
        ab_ref[1, q] = imag[:, part]
        ab_ref[2, q] = out[:, 512 + q * 128 : 512 + (q + 1) * 128]
    same = (iota((128, 128), 0) >> 5) == (iota((128, 128), 1) >> 5)
    for h in range(4):

        def gather(k):
            return jnp.concatenate(
                [
                    ab_ref[k, q, pl.ds(fl, 8, stride=FLOC), :]
                    for fl in range(4 * h, 4 * h + 4)
                    for q in range(4)
                ],
                axis=0,
            )

        b_hi, b_lo = split(jnp.where(same, gather(2), 0.0).T)
        a_hi, a_lo = split(jnp.concatenate([gather(0), gather(1)], axis=1))
        sub = (
            jnp.dot(b_hi, a_hi, preferred_element_type=F32)
            + jnp.dot(b_lo, a_hi, preferred_element_type=F32)
            + jnp.dot(b_hi, a_lo, preferred_element_type=F32)
        ) * (1.0 / FRAMES)
        sub = sub.astype(BF16)
        sall_ref[0, h * 128 : (h + 1) * 128, :] = sub[:, :128]
        sall_ref[1, h * 128 : (h + 1) * 128, :] = sub[:, 128:]


def image_chunk(chunk, sall_ref, t0_ref, ph_ref, ct_ref):
    part = slice(chunk * CHUNK, (chunk + 1) * CHUNK)
    table = t0_ref[:, part]
    g_r = jnp.dot(sall_ref[0], table, preferred_element_type=F32).reshape(FLOC, SUB, CHUNK)
    g_i = jnp.dot(sall_ref[1], table, preferred_element_type=F32).reshape(FLOC, SUB, CHUNK)
    cos = ph_ref[0, :, part][:, None, :]
    sin = ph_ref[1, :, part][:, None, :]
    p_r = (cos * g_r - sin * g_i).astype(BF16).reshape(FLOC * SUB, CHUNK)
    p_i = (cos * g_i + sin * g_r).astype(BF16).reshape(FLOC * SUB, CHUNK)
    image = jnp.dot(ct_ref[...], jnp.concatenate([p_r, p_i], axis=0), preferred_element_type=F32)
    return image.T


def kernel(
    v_hbm, flag_hbm, taps_hbm, kr_hbm, kc_hbm, cell_hbm, out_ref,
    v_ref, flag_ref, taps_ref, kr_ref, kc_ref, cell_ref,
    xs_ref, xr_ref, t0_ref, ph_ref, ct_ref, w_ref, ab_ref, sall_ref, img_ref,
    tr_ref, zs_ref, zr_ref, ys_ref, yr_ref,
    in_sem, near, mid, far, own_sem, a_send, a_recv, t_send, t_recv, z_send, z_recv, y_send, y_recv,
):
    role = lax.axis_index("role")
    band = lax.axis_index("band")
    mt = lax.axis_index("turn")
    y_lo = band // NZ
    mz = band % NZ
    my = 2 * role + y_lo

    def turn_of(k):
        return {"turn": (mt + 1 + k) % NT}

    def z_of(k):
        return {"band": y_lo * NZ + (mz + 1 + k) % NZ}

    def y_of(k):
        y = (my + 1 + k) % NY
        return {"role": y // 2, "band": (y % 2) * NZ + mz}

    def tell(sem, device):
        pl.semaphore_signal(sem, inc=1, device_id=device, device_id_type=MESH)

    fetches = [
        pltpu.make_async_copy(src, dst, in_sem.at[i])
        for i, (src, dst) in enumerate(
            (
                (v_hbm, v_ref), (taps_hbm, taps_ref), (flag_hbm, flag_ref),
                (kr_hbm, kr_ref), (kc_hbm, kc_ref), (cell_hbm, cell_ref),
            )
        )
    ]
    for fetch in fetches:
        fetch.start()

    barrier = pltpu.get_barrier_semaphore()
    for k in range(NT - 1):
        tell(barrier, turn_of(k))
    for step in (1, -1):
        tell(barrier, z_of(step - 1))
        tell(barrier, y_of(step - 1))

    for fetch in fetches[:3]:
        fetch.wait()
    channelize(v_ref, flag_ref, taps_ref, xs_ref)

    pl.semaphore_wait(barrier, NT + 3)
    spread = []
    for k in range(NT - 1):
        dest = (mt + 1 + k) % NT
        copy = pltpu.make_async_remote_copy(
            src_ref=xs_ref.at[dest], dst_ref=xr_ref.at[mt],
            send_sem=a_send.at[k], recv_sem=a_recv.at[mt],
            device_id=turn_of(k), device_id_type=MESH,
        )
        copy.start()
        spread.append(copy)
    own = pltpu.make_async_copy(xs_ref.at[mt], xr_ref.at[mt], own_sem)
    own.start()
    for step in (1, -1):
        tell(near, z_of(step - 1))
        tell(near, y_of(step - 1))

    for fetch in fetches[3:]:
        fetch.wait()
    tables(mt, my, mz, cell_ref, t0_ref, ph_ref, ct_ref)
    weights(kr_ref, kc_ref, w_ref)

    pl.semaphore_wait(near, 4)
    for step in (2, -2):
        tell(mid, z_of(step - 1))
        tell(mid, y_of(step - 1))

    own.wait()
    for k in range(NT - 1):
        src = (mt + 1 + k) % NT
        pltpu.make_async_remote_copy(
            src_ref=xs_ref.at[src], dst_ref=xr_ref.at[src],
            send_sem=a_send.at[k], recv_sem=a_recv.at[src],
            device_id=turn_of(k), device_id_type=MESH,
        ).wait_recv()

    pl.semaphore_wait(mid, 4)
    for step in (2, -2):
        tell(far, z_of(step - 1))

    subgrids(xr_ref, w_ref, ab_ref, sall_ref)

    def turn_copy(k):
        return pltpu.make_async_remote_copy(
            src_ref=img_ref.at[pl.ds(k * PIECE, PIECE), :], dst_ref=tr_ref.at[k],
            send_sem=t_send.at[k], recv_sem=t_recv.at[k],
            device_id=turn_of(k), device_id_type=MESH,
        )

    turn_copies = []
    done = 0
    for chunk in range(LW // CHUNK):
        rows = image_chunk(chunk, sall_ref, t0_ref, ph_ref, ct_ref)
        img_ref[chunk * CHUNK : (chunk + 1) * CHUNK, :] = rows.astype(BF16)
        while done < NT - 1 and (done + 1) * PIECE <= (chunk + 1) * CHUNK:
            copy = turn_copy(done)
            copy.start()
            turn_copies.append(copy)
            done += 1
    pl.semaphore_wait(far, 2)
    total = rows[CHUNK - PIECE :, :]
    for k in range(NT - 1):
        turn_copies[k].wait_recv()
        total = total + tr_ref[k].astype(F32)

    zs_ref[...] = total.astype(BF16).reshape(NZ, NY, MW)
    z_copies = []
    for k in range(NZ - 1):
        copy = pltpu.make_async_remote_copy(
            src_ref=zs_ref.at[k], dst_ref=zr_ref.at[k],
            send_sem=z_send.at[k], recv_sem=z_recv.at[k],
            device_id=z_of(k), device_id_type=MESH,
        )
        copy.start()
        z_copies.append(copy)
    total = total[(NZ - 1) * NY :, :]
    for k in range(NZ - 1):
        z_copies[k].wait_recv()
        total = total + zr_ref[k].astype(F32)

    y_copies = []
    for k in range(NY):
        ys_ref[k] = total[k : k + 1, :]
    for k in range(NY - 1):
        copy = pltpu.make_async_remote_copy(
            src_ref=ys_ref.at[k], dst_ref=yr_ref.at[k],
            send_sem=y_send.at[k], recv_sem=y_recv.at[k],
            device_id=y_of(k), device_id_type=MESH,
        )
        copy.start()
        y_copies.append(copy)
    final = total[NY - 1 : NY, :]
    for k in range(NY - 1):
        y_copies[k].wait_recv()
        final = final + yr_ref[k]
    out_ref[...] = final * SCALE
    for copy in spread + turn_copies + z_copies + y_copies:
        copy.wait_send()


def local(voltages, station_flags, filter_taps, kernel_rows, kernel_cols, cell_index):
    vmem = pl.BlockSpec(memory_space=pltpu.VMEM)
    hbm = pl.BlockSpec(memory_space=pl.ANY)
    dma = pltpu.SemaphoreType.DMA
    return pl.pallas_call(
        kernel,
        out_shape=jax.ShapeDtypeStruct((1, MW), F32),
        in_specs=[hbm] * 6,
        out_specs=vmem,
        scratch_shapes=[
            pltpu.VMEM((2 * STLOC, (FRAMES + TAPS - 1) * 2 * FINE), BF16),
            pltpu.SMEM((STLOC,), I32),
            pltpu.VMEM((TAPS * 2 * FINE, 2 * FINE), BF16),
            pltpu.VMEM((SUB, 256), BF16),
            pltpu.VMEM((SUB, 256), BF16),
            pltpu.SMEM((2, FLOC), I32),
            pltpu.VMEM((NT, 2, FLOC, 512), BF16),
            pltpu.VMEM((NT, 2, FLOC, 512), BF16),
            pltpu.VMEM((128, LW), BF16),
            pltpu.VMEM((2, FLOC, LW), F32),
            pltpu.VMEM((MW, 2 * FLOC * SUB), BF16),
            pltpu.VMEM((1024, 1024), BF16),
            pltpu.VMEM((3, 4, 128, 128), F32),
            pltpu.VMEM((2, FLOC * SUB, 128), BF16),
            pltpu.VMEM((LW, MW), BF16),
            pltpu.VMEM((NT - 1, PIECE, MW), BF16),
            pltpu.VMEM((NZ, NY, MW), BF16),
            pltpu.VMEM((NZ - 1, NY, MW), BF16),
            pltpu.VMEM((NY, 1, MW), F32),
            pltpu.VMEM((NY - 1, 1, MW), F32),
            dma((6,)),
            pltpu.SemaphoreType.REGULAR,
            pltpu.SemaphoreType.REGULAR,
            pltpu.SemaphoreType.REGULAR,
            dma,
            dma((NT - 1,)),
            dma((NT,)),
            dma((NT - 1,)),
            dma((NT - 1,)),
            dma((NZ - 1,)),
            dma((NZ - 1,)),
            dma((NY - 1,)),
            dma((NY - 1,)),
        ],
        compiler_params=pltpu.CompilerParams(collective_id=0, has_side_effects=True),
    )(
        voltages.reshape(2 * STLOC, -1),
        station_flags,
        filter_taps.reshape(TAPS * 2 * FINE, 2 * FINE),
        kernel_rows.reshape(SUB, -1),
        kernel_cols.reshape(SUB, -1),
        cell_index.reshape(2, FLOC),
    )


def solution(mesh):
    in_specs = (
        P(("role", "band"), None, "turn", None),
        P("turn"),
        P(),
        P(("role", "band"), None, None, None),
        P(("role", "band"), None, None, None),
        P(None, ("role", "band", "turn"), None),
    )
    out_specs = P(("role", "band", "turn"), None)
    return jax.shard_map(local, mesh=mesh, in_specs=in_specs, out_specs=out_specs, check_vma=False)
```

```python
import math

import jax
import jax.numpy as jnp
from jax import lax
from jax.experimental import pallas as pl
from jax.experimental.pallas import tpu as pltpu
from jax.sharding import PartitionSpec as P

MESH = pl.DeviceIdType.MESH
F32 = jnp.float32
BF16 = jnp.bfloat16
I32 = jnp.int32

NGRID = 4096
NT, NY, NZ = 8, 8, 12
FINE = 128
FLOC = 16
STLOC = 32
TAPS = 8
FRAMES = 8
SUB = 32
MW = 128
LW = NT * NY * NZ
PIECE = NY * NZ
SCALE = 4.0 / math.sqrt(96 * FINE * SUB * SUB)
CHUNK = 256
TURNS = ((2, 0), (2, 1), (1, 0), (1, 1), (3, 0), (3, 1), (0, 1), (0, 0))
ROWS_Z = (6, 5, 7, 4, 8, 3, 9, 2, 10, 1, 11, 0)
ROWS_Y = (4, 3, 5, 2, 6, 1, 7, 0)


def turn_at(mt, k):
    step, flip = TURNS[k]
    return (((mt >> 1) + step) & 3) * 2 + ((mt & 1) ^ flip)


def iota(shape, dim):
    return lax.broadcasted_iota(I32, shape, dim)


def trig(turns):
    shifted = turns + 512
    quadrant = shifted >> 10
    x = ((shifted & 1023) - 512).astype(F32) * (2.0 * math.pi / NGRID)
    x2 = x * x
    s = x * (1.0 + x2 * (-1.0 / 6 + x2 * (1.0 / 120 + x2 * (-1.0 / 5040 + x2 * (1.0 / 362880)))))
    c = 1.0 + x2 * (-0.5 + x2 * (1.0 / 24 + x2 * (-1.0 / 720 + x2 * (1.0 / 40320))))
    odd = (quadrant & 1) == 1
    cos = jnp.where(odd, s, c)
    sin = jnp.where(odd, c, s)
    cos = jnp.where(((quadrant + 1) & 2) == 2, -cos, cos)
    sin = jnp.where((quadrant & 2) == 2, -sin, sin)
    return cos, sin


def split(x):
    high = x.astype(BF16)
    return high, (x - high.astype(F32)).astype(BF16)


def channelize(v_ref, flag_ref, taps_ref, xs_ref):
    width = 2 * FINE
    lhs = jnp.concatenate(
        [v_ref[:, t * width : (t + TAPS) * width] for t in range(FRAMES)], axis=0
    )
    out = jnp.dot(lhs, taps_ref[...], preferred_element_type=F32)
    lane = iota((1, 128), 1) & (STLOC - 1)
    flags = jnp.zeros((1, 128), F32)
    for s in range(STLOC):
        flags = jnp.where(lane == s, flag_ref[s].astype(F32), flags)
    turned = out.astype(BF16).T * jnp.concatenate([flags] * 4, axis=1).astype(BF16)
    for d in range(NT):
        for c in range(2):
            xs_ref[d, c] = turned[c * FINE + d * FLOC : c * FINE + (d + 1) * FLOC, :]


def tables(mt, my, mz, cell_ref, t0_ref, ph_ref, ct_ref):
    lane = iota((1, LW), 1)
    kt = jnp.zeros((1, LW), I32)
    for i in range(1, NT):
        kt = kt + (lane >= PIECE * i).astype(I32)
    j = lane - PIECE * kt
    kz, ky = j >> 3, j & 7
    z = jnp.zeros((1, LW), I32) + mz
    for i, step in enumerate(ROWS_Z):
        z = jnp.where(kz == i, lax.rem(mz + step, NZ), z)
    y = jnp.zeros((1, LW), I32) + my
    for i, step in enumerate(ROWS_Y):
        y = jnp.where(ky == i, (my + step) & (NY - 1), y)
    t = jnp.zeros((1, LW), I32) + mt
    for i in range(NT):
        t = jnp.where(kt == i, turn_at(mt, i), t)
    pix = NT * (NZ * y + z) + t - LW // 2
    cos, sin = trig(iota((SUB, LW), 0) * pix)
    cos_hi, cos_lo = split(cos)
    sin_hi, sin_lo = split(sin)
    t0_ref[0:32] = cos_hi
    t0_ref[32:64] = sin_hi
    t0_ref[64:96] = cos_lo
    t0_ref[96:128] = sin_lo
    row = iota((FLOC, LW), 0)
    cell_u = jnp.zeros((FLOC, LW), I32)
    for n in range(FLOC):
        cell_u = jnp.where(row == n, cell_ref[0, n], cell_u)
    cos, sin = trig(cell_u * pix)
    ph_ref[0] = cos
    ph_ref[1] = sin
    lane = iota((1, FLOC * SUB), 1)
    cell_v = jnp.zeros((1, FLOC * SUB), I32)
    for n in range(FLOC):
        cell_v = jnp.where((lane >> 5) == n, cell_ref[1, n], cell_v)
    cell_v = cell_v + (lane & 31)
    cos, sin = trig((iota((MW, FLOC * SUB), 0) - MW // 2) * cell_v)
    ct_ref[:, : FLOC * SUB] = cos.astype(BF16)
    ct_ref[:, FLOC * SUB :] = (-sin).astype(BF16)


def weights(kr_ref, kc_ref, w_ref):
    w_ref[...] = jnp.zeros(w_ref.shape, BF16)
    for side, k_ref in enumerate((kr_ref, kc_ref)):
        k = k_ref[...].astype(F32)
        kt = jnp.concatenate([k] * 4, axis=0).T.astype(BF16)
        for src in range(NT):
            for q in range(4):
                w_ref[
                    src * 128 + q * 32 : src * 128 + (q + 1) * 32,
                    side * 512 + q * 128 : side * 512 + (q + 1) * 128,
                ] = kt[src * 32 : (src + 1) * 32, :]


def stations(chip, xr_ref, w_ref):
    lhs = jnp.concatenate(
        [
            jnp.concatenate(
                [xr_ref[2 * chip + core, c, :, g * 128 : (g + 1) * 128] for core in range(2)], axis=1
            )
            for g in range(4)
            for c in range(2)
        ],
        axis=0,
    )
    rows = pl.ds(pl.multiple_of(chip * 256, 256), 256)
    return jnp.dot(lhs, w_ref[rows, :], preferred_element_type=F32)


def subgrids(out, ab_ref, sall_ref):
    u = out[:, :512]
    v = jnp.concatenate(
        [
            u[(2 * g + 1) * FLOC : (2 * g + 2) * FLOC] if c == 0 else -u[2 * g * FLOC : (2 * g + 1) * FLOC]
            for g in range(4)
            for c in range(2)
        ],
        axis=0,
    )
    odd = ((iota((128, 512), 1) >> 5) & 1) == 1
    real = jnp.where(odd, -v, u)
    imag = jnp.where(odd, u, v)
    for q in range(4):
        part = slice(q * 128, (q + 1) * 128)
        ab_ref[0, q] = real[:, part]
        ab_ref[1, q] = imag[:, part]
        ab_ref[2, q] = out[:, 512 + q * 128 : 512 + (q + 1) * 128]
    same = (iota((128, 128), 0) >> 5) == (iota((128, 128), 1) >> 5)
    for h in range(4):

        def gather(k):
            return jnp.concatenate(
                [
                    ab_ref[k, q, pl.ds(fl, 8, stride=FLOC), :]
                    for fl in range(4 * h, 4 * h + 4)
                    for q in range(4)
                ],
                axis=0,
            )

        b_hi, b_lo = split(jnp.where(same, gather(2), 0.0).T)
        a_hi, a_lo = split(jnp.concatenate([gather(0), gather(1)], axis=1))
        sub = (
            jnp.dot(b_hi, a_hi, preferred_element_type=F32)
            + jnp.dot(b_lo, a_hi, preferred_element_type=F32)
            + jnp.dot(b_hi, a_lo, preferred_element_type=F32)
        ) * (1.0 / FRAMES)
        sub = sub.astype(BF16)
        sall_ref[0, h * 128 : (h + 1) * 128, :] = sub[:, :128]
        sall_ref[1, h * 128 : (h + 1) * 128, :] = sub[:, 128:]


def image_chunk(chunk, sall_ref, t0_ref, ph_ref, ct_ref):
    part = slice(chunk * CHUNK, (chunk + 1) * CHUNK)
    table = t0_ref[:, part]
    g_r = jnp.dot(sall_ref[0], table, preferred_element_type=F32).reshape(FLOC, SUB, CHUNK)
    g_i = jnp.dot(sall_ref[1], table, preferred_element_type=F32).reshape(FLOC, SUB, CHUNK)
    cos = ph_ref[0, :, part][:, None, :]
    sin = ph_ref[1, :, part][:, None, :]
    p_r = (cos * g_r - sin * g_i).astype(BF16).reshape(FLOC * SUB, CHUNK)
    p_i = (cos * g_i + sin * g_r).astype(BF16).reshape(FLOC * SUB, CHUNK)
    image = jnp.dot(ct_ref[...], jnp.concatenate([p_r, p_i], axis=0), preferred_element_type=F32)
    return image.T


def kernel(
    v_hbm, flag_hbm, taps_hbm, kr_hbm, kc_hbm, cell_hbm, out_ref,
    v_ref, flag_ref, taps_ref, kr_ref, kc_ref, cell_ref,
    xs_ref, xr_ref, t0_ref, ph_ref, ct_ref, w_ref, ab_ref, sall_ref, img_ref,
    tr_ref, zs_ref, zr_ref, ys_ref, yr_ref,
    in_sem, near, mid, far, own_sem, a_send, a_recv, t_send, t_recv, z_send, z_recv, y_send, y_recv,
):
    role = lax.axis_index("role")
    band = lax.axis_index("band")
    mt = lax.axis_index("turn")
    y_lo = (band >= NZ).astype(I32)
    mz = band - NZ * y_lo
    my = 2 * role + y_lo

    def turn_of(k):
        return {"turn": turn_at(mt, k)}

    def z_of(step):
        return {"band": y_lo * NZ + lax.rem(mz + step, NZ)}

    def y_of(step):
        y = (my + step) & (NY - 1)
        return {"role": y >> 1, "band": (y & 1) * NZ + mz}

    def tell(sem, device):
        pl.semaphore_signal(sem, inc=1, device_id=device, device_id_type=MESH)

    fetches = [
        pltpu.make_async_copy(src, dst, in_sem.at[i])
        for i, (src, dst) in enumerate(
            (
                (v_hbm, v_ref), (taps_hbm, taps_ref), (flag_hbm, flag_ref),
                (kr_hbm, kr_ref), (kc_hbm, kc_ref), (cell_hbm, cell_ref),
            )
        )
    ]
    for fetch in fetches:
        fetch.start()

    barrier = pltpu.get_barrier_semaphore()
    for k in range(NT - 1):
        tell(barrier, turn_of(k))
    for step in (1, -1):
        tell(barrier, z_of(step + NZ))
        tell(barrier, y_of(step))

    for fetch in fetches[:3]:
        fetch.wait()
    channelize(v_ref, flag_ref, taps_ref, xs_ref)

    pl.semaphore_wait(barrier, NT + 3)
    spread = []
    for k in range(NT - 1):
        dest = turn_at(mt, k)
        copy = pltpu.make_async_remote_copy(
            src_ref=xs_ref.at[dest], dst_ref=xr_ref.at[mt],
            send_sem=a_send.at[k], recv_sem=a_recv.at[mt],
            device_id=turn_of(k), device_id_type=MESH,
        )
        copy.start()
        spread.append(copy)
    own = pltpu.make_async_copy(xs_ref.at[mt], xr_ref.at[mt], own_sem)
    own.start()
    for step in (1, -1):
        tell(near, z_of(step + NZ))
        tell(near, y_of(step))

    for fetch in fetches[3:]:
        fetch.wait()
    tables(mt, my, mz, cell_ref, t0_ref, ph_ref, ct_ref)
    weights(kr_ref, kc_ref, w_ref)

    pl.semaphore_wait(near, 4)
    for step in (2, -2):
        tell(mid, z_of(step + NZ))
        tell(mid, y_of(step))

    own.wait()

    def arrived(k):
        src = turn_at(mt, k)
        pltpu.make_async_remote_copy(
            src_ref=xs_ref.at[src], dst_ref=xr_ref.at[src],
            send_sem=a_send.at[k], recv_sem=a_recv.at[src],
            device_id=turn_of(k), device_id_type=MESH,
        ).wait_recv()

    out = None
    for group in ((6,), (2, 3), (4, 5), (0, 1)):
        for k in group:
            arrived(k)
        term = stations(turn_at(mt, group[0]) >> 1, xr_ref, w_ref)
        out = term if out is None else out + term

    pl.semaphore_wait(mid, 4)
    for step in (2, -2):
        tell(far, z_of(step + NZ))

    subgrids(out, ab_ref, sall_ref)

    def turn_copy(k):
        return pltpu.make_async_remote_copy(
            src_ref=img_ref.at[pl.ds(k * PIECE, PIECE), :], dst_ref=tr_ref.at[k],
            send_sem=t_send.at[k], recv_sem=t_recv.at[k],
            device_id=turn_of(k), device_id_type=MESH,
        )

    turn_copies = []
    done = 0
    for chunk in range(LW // CHUNK):
        rows = image_chunk(chunk, sall_ref, t0_ref, ph_ref, ct_ref)
        img_ref[chunk * CHUNK : (chunk + 1) * CHUNK, :] = rows.astype(BF16)
        while done < NT - 1 and (done + 1) * PIECE <= (chunk + 1) * CHUNK:
            copy = turn_copy(done)
            copy.start()
            turn_copies.append(copy)
            done += 1
    pl.semaphore_wait(far, 2)
    total = rows[CHUNK - PIECE :, :]
    for k in range(NT - 1):
        turn_copies[k].wait_recv()
        total = total + tr_ref[k].astype(F32)

    zs_ref[...] = total.astype(BF16).reshape(NZ, NY, MW)
    z_copies = []
    for k in range(NZ - 1):
        copy = pltpu.make_async_remote_copy(
            src_ref=zs_ref.at[k], dst_ref=zr_ref.at[k],
            send_sem=z_send.at[k], recv_sem=z_recv.at[k],
            device_id=z_of(ROWS_Z[k]), device_id_type=MESH,
        )
        copy.start()
        z_copies.append(copy)
    total = total[(NZ - 1) * NY :, :]
    for k in range(NZ - 1):
        z_copies[k].wait_recv()
        total = total + zr_ref[k].astype(F32)

    y_copies = []
    for k in range(NY):
        ys_ref[k] = total[k : k + 1, :]
    for k in range(NY - 1):
        copy = pltpu.make_async_remote_copy(
            src_ref=ys_ref.at[k], dst_ref=yr_ref.at[k],
            send_sem=y_send.at[k], recv_sem=y_recv.at[k],
            device_id=y_of(ROWS_Y[k]), device_id_type=MESH,
        )
        copy.start()
        y_copies.append(copy)
    final = total[NY - 1 : NY, :]
    for k in range(NY - 1):
        y_copies[k].wait_recv()
        final = final + yr_ref[k]
    out_ref[...] = final * SCALE
    for copy in spread + turn_copies + z_copies + y_copies:
        copy.wait_send()


def local(voltages, station_flags, filter_taps, kernel_rows, kernel_cols, cell_index):
    vmem = pl.BlockSpec(memory_space=pltpu.VMEM)
    hbm = pl.BlockSpec(memory_space=pl.ANY)
    dma = pltpu.SemaphoreType.DMA
    return pl.pallas_call(
        kernel,
        out_shape=jax.ShapeDtypeStruct((1, MW), F32),
        in_specs=[hbm] * 6,
        out_specs=vmem,
        scratch_shapes=[
            pltpu.VMEM((2 * STLOC, (FRAMES + TAPS - 1) * 2 * FINE), BF16),
            pltpu.SMEM((STLOC,), I32),
            pltpu.VMEM((TAPS * 2 * FINE, 2 * FINE), BF16),
            pltpu.VMEM((SUB, 256), BF16),
            pltpu.VMEM((SUB, 256), BF16),
            pltpu.SMEM((2, FLOC), I32),
            pltpu.VMEM((NT, 2, FLOC, 512), BF16),
            pltpu.VMEM((NT, 2, FLOC, 512), BF16),
            pltpu.VMEM((128, LW), BF16),
            pltpu.VMEM((2, FLOC, LW), F32),
            pltpu.VMEM((MW, 2 * FLOC * SUB), BF16),
            pltpu.VMEM((1024, 1024), BF16),
            pltpu.VMEM((3, 4, 128, 128), F32),
            pltpu.VMEM((2, FLOC * SUB, 128), BF16),
            pltpu.VMEM((LW, MW), BF16),
            pltpu.VMEM((NT - 1, PIECE, MW), BF16),
            pltpu.VMEM((NZ, NY, MW), BF16),
            pltpu.VMEM((NZ - 1, NY, MW), BF16),
            pltpu.VMEM((NY, 1, MW), F32),
            pltpu.VMEM((NY - 1, 1, MW), F32),
            dma((6,)),
            pltpu.SemaphoreType.REGULAR,
            pltpu.SemaphoreType.REGULAR,
            pltpu.SemaphoreType.REGULAR,
            dma,
            dma((NT - 1,)),
            dma((NT,)),
            dma((NT - 1,)),
            dma((NT - 1,)),
            dma((NZ - 1,)),
            dma((NZ - 1,)),
            dma((NY - 1,)),
            dma((NY - 1,)),
        ],
        compiler_params=pltpu.CompilerParams(collective_id=0, has_side_effects=True, vmem_limit_bytes=24 << 20),
    )(
        pltpu.with_memory_space_constraint(voltages.reshape(2 * STLOC, -1), pltpu.HBM),
        pltpu.with_memory_space_constraint(station_flags, pltpu.HBM),
        pltpu.with_memory_space_constraint(filter_taps.reshape(TAPS * 2 * FINE, 2 * FINE), pltpu.HBM),
        pltpu.with_memory_space_constraint(kernel_rows.reshape(SUB, -1), pltpu.HBM),
        pltpu.with_memory_space_constraint(kernel_cols.reshape(SUB, -1), pltpu.HBM),
        pltpu.with_memory_space_constraint(cell_index.reshape(2, FLOC), pltpu.HBM),
    )


def solution(mesh):
    in_specs = (
        P(("role", "band"), None, "turn", None),
        P("turn"),
        P(),
        P(("role", "band"), None, None, None),
        P(("role", "band"), None, None, None),
        P(None, ("role", "band", "turn"), None),
    )
    out_specs = P(("role", "band", "turn"), None)
    return jax.shard_map(local, mesh=mesh, in_specs=in_specs, out_specs=out_specs, check_vma=False)
```

```python
import math

import jax
import jax.numpy as jnp
from jax import lax
from jax.experimental import pallas as pl
from jax.experimental.pallas import tpu as pltpu
from jax.sharding import PartitionSpec as P

MESH = pl.DeviceIdType.MESH
F32 = jnp.float32
BF16 = jnp.bfloat16
I32 = jnp.int32

NGRID = 4096
NT, NY, NZ = 8, 8, 12
FINE = 128
FLOC = 16
STLOC = 32
TAPS = 8
FRAMES = 8
SUB = 32
MW = 128
LW = NT * NY * NZ
PIECE = NY * NZ
SCALE = 4.0 / math.sqrt(96 * FINE * SUB * SUB)
EDGES = (0, 128, 384, 768)
TURNS = ((2, 0), (2, 1), (1, 0), (1, 1), (3, 0), (3, 1), (0, 1), (0, 0))
ROWS_Z = (6, 5, 7, 4, 8, 3, 9, 2, 10, 1, 11, 0)
ROWS_Y = (4, 3, 5, 2, 6, 1, 7, 0)


def turn_at(mt, k):
    step, flip = TURNS[k]
    return (((mt >> 1) + step) & 3) * 2 + ((mt & 1) ^ flip)


def iota(shape, dim):
    return lax.broadcasted_iota(I32, shape, dim)


def trig(turns):
    shifted = turns + 512
    quadrant = shifted >> 10
    x = ((shifted & 1023) - 512).astype(F32) * (2.0 * math.pi / NGRID)
    x2 = x * x
    s = x * (1.0 + x2 * (-1.0 / 6 + x2 * (1.0 / 120 + x2 * (-1.0 / 5040 + x2 * (1.0 / 362880)))))
    c = 1.0 + x2 * (-0.5 + x2 * (1.0 / 24 + x2 * (-1.0 / 720 + x2 * (1.0 / 40320))))
    odd = (quadrant & 1) == 1
    cos = jnp.where(odd, s, c)
    sin = jnp.where(odd, c, s)
    cos = jnp.where(((quadrant + 1) & 2) == 2, -cos, cos)
    sin = jnp.where((quadrant & 2) == 2, -sin, sin)
    return cos, sin


def split(x):
    high = x.astype(BF16)
    return high, (x - high.astype(F32)).astype(BF16)


def channelize(v_ref, flag_ref, taps_ref, xs_ref):
    width = 2 * FINE
    lhs = jnp.concatenate(
        [v_ref[:, t * width : (t + TAPS) * width] for t in range(FRAMES)], axis=0
    )
    out = jnp.dot(lhs, taps_ref[...], preferred_element_type=F32)
    lane = iota((1, 128), 1) & (STLOC - 1)
    flags = jnp.zeros((1, 128), F32)
    for s in range(STLOC):
        flags = jnp.where(lane == s, flag_ref[s].astype(F32), flags)
    turned = out.astype(BF16).T * jnp.concatenate([flags] * 4, axis=1).astype(BF16)
    for d in range(NT):
        for c in range(2):
            xs_ref[d, c] = turned[c * FINE + d * FLOC : c * FINE + (d + 1) * FLOC, :]


def tables(mt, my, mz, cell_ref, t0_ref, ph_ref, ct_ref):
    lane = iota((1, LW), 1)
    kt = jnp.zeros((1, LW), I32)
    for i in range(1, NT):
        kt = kt + (lane >= PIECE * i).astype(I32)
    j = lane - PIECE * kt
    kz, ky = j >> 3, j & 7
    z = jnp.zeros((1, LW), I32) + mz
    for i, step in enumerate(ROWS_Z):
        z = jnp.where(kz == i, lax.rem(mz + step, NZ), z)
    y = jnp.zeros((1, LW), I32) + my
    for i, step in enumerate(ROWS_Y):
        y = jnp.where(ky == i, (my + step) & (NY - 1), y)
    t = jnp.zeros((1, LW), I32) + mt
    for i in range(NT):
        t = jnp.where(kt == i, turn_at(mt, i), t)
    pix = NT * (NZ * y + z) + t - LW // 2
    cos, sin = trig(iota((SUB, LW), 0) * pix)
    cos_hi, cos_lo = split(cos)
    sin_hi, sin_lo = split(sin)
    t0_ref[0:32] = cos_hi
    t0_ref[32:64] = sin_hi
    t0_ref[64:96] = cos_lo
    t0_ref[96:128] = sin_lo
    row = iota((FLOC, LW), 0)
    cell_u = jnp.zeros((FLOC, LW), I32)
    for n in range(FLOC):
        cell_u = jnp.where(row == n, cell_ref[0, n], cell_u)
    cos, sin = trig(cell_u * pix)
    ph_ref[0] = cos
    ph_ref[1] = sin
    lane = iota((1, FLOC * SUB), 1)
    cell_v = jnp.zeros((1, FLOC * SUB), I32)
    for n in range(FLOC):
        cell_v = jnp.where((lane >> 5) == n, cell_ref[1, n], cell_v)
    cell_v = cell_v + (lane & 31)
    cos, sin = trig((iota((MW, FLOC * SUB), 0) - MW // 2) * cell_v)
    ct_ref[:, : FLOC * SUB] = cos.astype(BF16)
    ct_ref[:, FLOC * SUB :] = (-sin).astype(BF16)


def weights(kr_ref, kc_ref, w_ref):
    w_ref[...] = jnp.zeros(w_ref.shape, BF16)
    for side, k_ref in enumerate((kr_ref, kc_ref)):
        k = k_ref[...].astype(F32)
        kt = jnp.concatenate([k] * 4, axis=0).T.astype(BF16)
        for src in range(NT):
            for q in range(4):
                w_ref[
                    src * 128 + q * 32 : src * 128 + (q + 1) * 32,
                    side * 512 + q * 128 : side * 512 + (q + 1) * 128,
                ] = kt[src * 32 : (src + 1) * 32, :]


def stations(chip, xr_ref, w_ref):
    lhs = jnp.concatenate(
        [
            jnp.concatenate(
                [xr_ref[2 * chip + core, c, :, g * 128 : (g + 1) * 128] for core in range(2)], axis=1
            )
            for g in range(4)
            for c in range(2)
        ],
        axis=0,
    )
    rows = pl.ds(pl.multiple_of(chip * 256, 256), 256)
    return jnp.dot(lhs, w_ref[rows, :], preferred_element_type=F32)


def subgrids(out, ab_ref, sall_ref):
    u = out[:, :512]
    v = jnp.concatenate(
        [
            u[(2 * g + 1) * FLOC : (2 * g + 2) * FLOC] if c == 0 else -u[2 * g * FLOC : (2 * g + 1) * FLOC]
            for g in range(4)
            for c in range(2)
        ],
        axis=0,
    )
    odd = ((iota((128, 512), 1) >> 5) & 1) == 1
    real = jnp.where(odd, -v, u)
    imag = jnp.where(odd, u, v)
    for q in range(4):
        part = slice(q * 128, (q + 1) * 128)
        ab_ref[0, q] = real[:, part]
        ab_ref[1, q] = imag[:, part]
        ab_ref[2, q] = out[:, 512 + q * 128 : 512 + (q + 1) * 128]
    same = (iota((128, 128), 0) >> 5) == (iota((128, 128), 1) >> 5)
    for h in range(4):

        def gather(k):
            return jnp.concatenate(
                [
                    ab_ref[k, q, pl.ds(fl, 8, stride=FLOC), :]
                    for fl in range(4 * h, 4 * h + 4)
                    for q in range(4)
                ],
                axis=0,
            )

        b_hi, b_lo = split(jnp.where(same, gather(2), 0.0).T)
        a_hi, a_lo = split(jnp.concatenate([gather(0), gather(1)], axis=1))
        sub = (
            jnp.dot(b_hi, a_hi, preferred_element_type=F32)
            + jnp.dot(b_lo, a_hi, preferred_element_type=F32)
            + jnp.dot(b_hi, a_lo, preferred_element_type=F32)
        ) * (1.0 / FRAMES)
        sub = sub.astype(BF16)
        sall_ref[0, h * 128 : (h + 1) * 128, :] = sub[:, :128]
        sall_ref[1, h * 128 : (h + 1) * 128, :] = sub[:, 128:]


def image_chunk(start, stop, sall_ref, t0_ref, ph_ref, ct_ref):
    width = stop - start
    part = slice(start, stop)
    table = t0_ref[:, part]
    g_r = jnp.dot(sall_ref[0], table, preferred_element_type=F32).reshape(FLOC, SUB, width)
    g_i = jnp.dot(sall_ref[1], table, preferred_element_type=F32).reshape(FLOC, SUB, width)
    cos = ph_ref[0, :, part][:, None, :]
    sin = ph_ref[1, :, part][:, None, :]
    p_r = (cos * g_r - sin * g_i).astype(BF16).reshape(FLOC * SUB, width)
    p_i = (cos * g_i + sin * g_r).astype(BF16).reshape(FLOC * SUB, width)
    image = jnp.dot(ct_ref[...], jnp.concatenate([p_r, p_i], axis=0), preferred_element_type=F32)
    return image.T


def kernel(
    v_hbm, flag_hbm, taps_hbm, kr_hbm, kc_hbm, cell_hbm, out_ref,
    v_ref, flag_ref, taps_ref, kr_ref, kc_ref, cell_ref,
    xs_ref, xr_ref, t0_ref, ph_ref, ct_ref, w_ref, ab_ref, sall_ref, img_ref,
    tr_ref, zs_ref, zr_ref, ys_ref, yr_ref,
    in_sem, near, mid, far, own_sem, a_send, a_recv, t_send, t_recv, z_send, z_recv, y_send, y_recv,
):
    role = lax.axis_index("role")
    band = lax.axis_index("band")
    mt = lax.axis_index("turn")
    y_lo = (band >= NZ).astype(I32)
    mz = band - NZ * y_lo
    my = 2 * role + y_lo

    def turn_of(k):
        return {"turn": turn_at(mt, k)}

    def z_of(step):
        return {"band": y_lo * NZ + lax.rem(mz + step, NZ)}

    def y_of(step):
        y = (my + step) & (NY - 1)
        return {"role": y >> 1, "band": (y & 1) * NZ + mz}

    def tell(sem, device):
        pl.semaphore_signal(sem, inc=1, device_id=device, device_id_type=MESH)

    fetches = [
        pltpu.make_async_copy(src, dst, in_sem.at[i])
        for i, (src, dst) in enumerate(
            (
                (v_hbm, v_ref), (taps_hbm, taps_ref), (flag_hbm, flag_ref),
                (kr_hbm, kr_ref), (kc_hbm, kc_ref), (cell_hbm, cell_ref),
            )
        )
    ]
    for fetch in fetches:
        fetch.start()

    barrier = pltpu.get_barrier_semaphore()
    for k in range(NT - 1):
        tell(barrier, turn_of(k))
    for step in (1, -1):
        tell(barrier, z_of(step + NZ))
        tell(barrier, y_of(step))

    for fetch in fetches[:3]:
        fetch.wait()
    channelize(v_ref, flag_ref, taps_ref, xs_ref)

    pl.semaphore_wait(barrier, NT + 3)
    spread = []
    for k in range(NT - 1):
        dest = turn_at(mt, k)
        copy = pltpu.make_async_remote_copy(
            src_ref=xs_ref.at[dest], dst_ref=xr_ref.at[mt],
            send_sem=a_send.at[k], recv_sem=a_recv.at[mt],
            device_id=turn_of(k), device_id_type=MESH,
        )
        copy.start()
        spread.append(copy)
    own = pltpu.make_async_copy(xs_ref.at[mt], xr_ref.at[mt], own_sem)
    own.start()
    for step in (1, -1):
        tell(near, z_of(step + NZ))
        tell(near, y_of(step))

    for fetch in fetches[3:]:
        fetch.wait()
    tables(mt, my, mz, cell_ref, t0_ref, ph_ref, ct_ref)
    weights(kr_ref, kc_ref, w_ref)

    pl.semaphore_wait(near, 4)
    for step in (2, -2):
        tell(mid, z_of(step + NZ))
        tell(mid, y_of(step))

    own.wait()

    def arrived(k):
        src = turn_at(mt, k)
        pltpu.make_async_remote_copy(
            src_ref=xs_ref.at[src], dst_ref=xr_ref.at[src],
            send_sem=a_send.at[k], recv_sem=a_recv.at[src],
            device_id=turn_of(k), device_id_type=MESH,
        ).wait_recv()

    out = None
    for group in ((6,), (2, 3), (4, 5), (0, 1)):
        for k in group:
            arrived(k)
        term = stations(turn_at(mt, group[0]) >> 1, xr_ref, w_ref)
        out = term if out is None else out + term

    pl.semaphore_wait(mid, 4)
    for step in (2, -2):
        tell(far, z_of(step + NZ))

    subgrids(out, ab_ref, sall_ref)

    def turn_copy(k):
        return pltpu.make_async_remote_copy(
            src_ref=img_ref.at[pl.ds(k * PIECE, PIECE), :], dst_ref=tr_ref.at[k],
            send_sem=t_send.at[k], recv_sem=t_recv.at[k],
            device_id=turn_of(k), device_id_type=MESH,
        )

    turn_copies = []
    done = 0
    for start, stop in zip(EDGES, EDGES[1:]):
        rows = image_chunk(start, stop, sall_ref, t0_ref, ph_ref, ct_ref)
        img_ref[start:stop, :] = rows.astype(BF16)
        while done < NT - 1 and (done + 1) * PIECE <= stop:
            copy = turn_copy(done)
            copy.start()
            turn_copies.append(copy)
            done += 1
    pl.semaphore_wait(far, 2)
    total = rows[rows.shape[0] - PIECE :, :]
    for k in range(NT - 1):
        turn_copies[k].wait_recv()
        total = total + tr_ref[k].astype(F32)

    zs_ref[...] = total.astype(BF16).reshape(NZ, NY, MW)
    z_copies = []
    for k in range(NZ - 1):
        copy = pltpu.make_async_remote_copy(
            src_ref=zs_ref.at[k], dst_ref=zr_ref.at[k],
            send_sem=z_send.at[k], recv_sem=z_recv.at[k],
            device_id=z_of(ROWS_Z[k]), device_id_type=MESH,
        )
        copy.start()
        z_copies.append(copy)
    total = total[(NZ - 1) * NY :, :]
    for k in range(NZ - 1):
        z_copies[k].wait_recv()
        total = total + zr_ref[k].astype(F32)

    y_copies = []
    for k in range(NY):
        ys_ref[k] = total[k : k + 1, :]
    for k in range(NY - 1):
        copy = pltpu.make_async_remote_copy(
            src_ref=ys_ref.at[k], dst_ref=yr_ref.at[k],
            send_sem=y_send.at[k], recv_sem=y_recv.at[k],
            device_id=y_of(ROWS_Y[k]), device_id_type=MESH,
        )
        copy.start()
        y_copies.append(copy)
    final = total[NY - 1 : NY, :]
    for k in range(NY - 1):
        y_copies[k].wait_recv()
        final = final + yr_ref[k]
    out_ref[...] = final * SCALE
    for copy in spread + turn_copies + z_copies + y_copies:
        copy.wait_send()


def local(voltages, station_flags, filter_taps, kernel_rows, kernel_cols, cell_index):
    vmem = pl.BlockSpec(memory_space=pltpu.VMEM)
    hbm = pl.BlockSpec(memory_space=pl.ANY)
    dma = pltpu.SemaphoreType.DMA
    return pl.pallas_call(
        kernel,
        out_shape=jax.ShapeDtypeStruct((1, MW), F32),
        in_specs=[hbm] * 6,
        out_specs=vmem,
        scratch_shapes=[
            pltpu.VMEM((2 * STLOC, (FRAMES + TAPS - 1) * 2 * FINE), BF16),
            pltpu.SMEM((STLOC,), I32),
            pltpu.VMEM((TAPS * 2 * FINE, 2 * FINE), BF16),
            pltpu.VMEM((SUB, 256), BF16),
            pltpu.VMEM((SUB, 256), BF16),
            pltpu.SMEM((2, FLOC), I32),
            pltpu.VMEM((NT, 2, FLOC, 512), BF16),
            pltpu.VMEM((NT, 2, FLOC, 512), BF16),
            pltpu.VMEM((128, LW), BF16),
            pltpu.VMEM((2, FLOC, LW), F32),
            pltpu.VMEM((MW, 2 * FLOC * SUB), BF16),
            pltpu.VMEM((1024, 1024), BF16),
            pltpu.VMEM((3, 4, 128, 128), F32),
            pltpu.VMEM((2, FLOC * SUB, 128), BF16),
            pltpu.VMEM((LW, MW), BF16),
            pltpu.VMEM((NT - 1, PIECE, MW), BF16),
            pltpu.VMEM((NZ, NY, MW), BF16),
            pltpu.VMEM((NZ - 1, NY, MW), BF16),
            pltpu.VMEM((NY, 1, MW), F32),
            pltpu.VMEM((NY - 1, 1, MW), F32),
            dma((6,)),
            pltpu.SemaphoreType.REGULAR,
            pltpu.SemaphoreType.REGULAR,
            pltpu.SemaphoreType.REGULAR,
            dma,
            dma((NT - 1,)),
            dma((NT,)),
            dma((NT - 1,)),
            dma((NT - 1,)),
            dma((NZ - 1,)),
            dma((NZ - 1,)),
            dma((NY - 1,)),
            dma((NY - 1,)),
        ],
        compiler_params=pltpu.CompilerParams(collective_id=0, has_side_effects=True, vmem_limit_bytes=24 << 20),
    )(
        pltpu.with_memory_space_constraint(voltages.reshape(2 * STLOC, -1), pltpu.HBM),
        pltpu.with_memory_space_constraint(station_flags, pltpu.HBM),
        pltpu.with_memory_space_constraint(filter_taps.reshape(TAPS * 2 * FINE, 2 * FINE), pltpu.HBM),
        pltpu.with_memory_space_constraint(kernel_rows.reshape(SUB, -1), pltpu.HBM),
        pltpu.with_memory_space_constraint(kernel_cols.reshape(SUB, -1), pltpu.HBM),
        pltpu.with_memory_space_constraint(cell_index.reshape(2, FLOC), pltpu.HBM),
    )


def solution(mesh):
    in_specs = (
        P(("role", "band"), None, "turn", None),
        P("turn"),
        P(),
        P(("role", "band"), None, None, None),
        P(("role", "band"), None, None, None),
        P(None, ("role", "band", "turn"), None),
    )
    out_specs = P(("role", "band", "turn"), None)
    return jax.shard_map(local, mesh=mesh, in_specs=in_specs, out_specs=out_specs, check_vma=False)
```

```python
import math

import jax
import jax.numpy as jnp
from jax import lax
from jax.experimental import pallas as pl
from jax.experimental.pallas import tpu as pltpu
from jax.sharding import PartitionSpec as P

MESH = pl.DeviceIdType.MESH
F32 = jnp.float32
BF16 = jnp.bfloat16
I32 = jnp.int32

NGRID = 4096
NT, NY, NZ = 8, 8, 12
FINE = 128
FLOC = 16
STLOC = 32
TAPS = 8
FRAMES = 8
SUB = 32
MW = 128
LW = NT * NY * NZ
PIECE = NY * NZ
SCALE = 4.0 / math.sqrt(96 * FINE * SUB * SUB)
EDGES = (0, 128, 384, 768)
TURNS = ((2, 0), (2, 1), (1, 0), (1, 1), (3, 0), (3, 1), (0, 1), (0, 0))
ROWS_Z = (6, 5, 7, 4, 8, 3, 9, 2, 10, 1, 11, 0)
ROWS_Y = (4, 3, 5, 2, 6, 1, 7, 0)


def turn_at(mt, k):
    step, flip = TURNS[k]
    return (((mt >> 1) + step) & 3) * 2 + ((mt & 1) ^ flip)


def iota(shape, dim):
    return lax.broadcasted_iota(I32, shape, dim)


def trig(turns):
    shifted = turns + 512
    quadrant = shifted >> 10
    x = ((shifted & 1023) - 512).astype(F32) * (2.0 * math.pi / NGRID)
    x2 = x * x
    s = x * (1.0 + x2 * (-1.0 / 6 + x2 * (1.0 / 120 + x2 * (-1.0 / 5040 + x2 * (1.0 / 362880)))))
    c = 1.0 + x2 * (-0.5 + x2 * (1.0 / 24 + x2 * (-1.0 / 720 + x2 * (1.0 / 40320))))
    odd = (quadrant & 1) == 1
    cos = jnp.where(odd, s, c)
    sin = jnp.where(odd, c, s)
    cos = jnp.where(((quadrant + 1) & 2) == 2, -cos, cos)
    sin = jnp.where((quadrant & 2) == 2, -sin, sin)
    return cos, sin


def split(x):
    high = x.astype(BF16)
    return high, (x - high.astype(F32)).astype(BF16)


def channelize(v_ref, flag_ref, taps_ref, xs_ref):
    width = 2 * FINE
    lhs = jnp.concatenate(
        [v_ref[:, t * width : (t + TAPS) * width] for t in range(FRAMES)], axis=0
    )
    out = jnp.dot(lhs, taps_ref[...], preferred_element_type=F32)
    lane = iota((1, 128), 1) & (STLOC - 1)
    flags = jnp.zeros((1, 128), F32)
    for s in range(STLOC):
        flags = jnp.where(lane == s, flag_ref[s].astype(F32), flags)
    turned = out.astype(BF16).T * jnp.concatenate([flags] * 4, axis=1).astype(BF16)
    for d in range(NT):
        for c in range(2):
            xs_ref[d, c] = turned[c * FINE + d * FLOC : c * FINE + (d + 1) * FLOC, :]


def tables(mt, my, mz, cell_ref, t0_ref, ph_ref, ct_ref):
    lane = iota((1, LW), 1)
    kt = jnp.zeros((1, LW), I32)
    for i in range(1, NT):
        kt = kt + (lane >= PIECE * i).astype(I32)
    j = lane - PIECE * kt
    kz, ky = j >> 3, j & 7
    z = jnp.zeros((1, LW), I32) + mz
    for i, step in enumerate(ROWS_Z):
        z = jnp.where(kz == i, lax.rem(mz + step, NZ), z)
    y = jnp.zeros((1, LW), I32) + my
    for i, step in enumerate(ROWS_Y):
        y = jnp.where(ky == i, (my + step) & (NY - 1), y)
    t = jnp.zeros((1, LW), I32) + mt
    for i in range(NT):
        t = jnp.where(kt == i, turn_at(mt, i), t)
    pix = NT * (NZ * y + z) + t - LW // 2
    cos, sin = trig(iota((SUB, LW), 0) * pix)
    cos_hi, cos_lo = split(cos)
    sin_hi, sin_lo = split(sin)
    t0_ref[0:32] = cos_hi
    t0_ref[32:64] = sin_hi
    t0_ref[64:96] = cos_lo
    t0_ref[96:128] = sin_lo
    row = iota((FLOC, LW), 0)
    cell_u = jnp.zeros((FLOC, LW), I32)
    for n in range(FLOC):
        cell_u = jnp.where(row == n, cell_ref[0, n], cell_u)
    cos, sin = trig(cell_u * pix)
    ph_ref[0] = cos
    ph_ref[1] = sin
    lane = iota((1, FLOC * SUB), 1)
    cell_v = jnp.zeros((1, FLOC * SUB), I32)
    for n in range(FLOC):
        cell_v = jnp.where((lane >> 5) == n, cell_ref[1, n], cell_v)
    cell_v = cell_v + (lane & 31)
    cos, sin = trig((iota((MW, FLOC * SUB), 0) - MW // 2) * cell_v)
    ct_ref[:, : FLOC * SUB] = cos.astype(BF16)
    ct_ref[:, FLOC * SUB :] = (-sin).astype(BF16)


def weights(kr_ref, kc_ref, w_ref):
    w_ref[...] = jnp.zeros(w_ref.shape, BF16)
    for side, k_ref in enumerate((kr_ref, kc_ref)):
        k = k_ref[...].astype(F32)
        kt = jnp.concatenate([k] * 4, axis=0).T.astype(BF16)
        for src in range(NT):
            for q in range(4):
                w_ref[
                    src * 128 + q * 32 : src * 128 + (q + 1) * 32,
                    side * 512 + q * 128 : side * 512 + (q + 1) * 128,
                ] = kt[src * 32 : (src + 1) * 32, :]


def stations(chip, xr_ref, w_ref):
    lhs = jnp.concatenate(
        [
            jnp.concatenate(
                [xr_ref[2 * chip + core, c, :, g * 128 : (g + 1) * 128] for core in range(2)], axis=1
            )
            for g in range(4)
            for c in range(2)
        ],
        axis=0,
    )
    rows = pl.ds(pl.multiple_of(chip * 256, 256), 256)
    return jnp.dot(lhs, w_ref[rows, :], preferred_element_type=F32)


def subgrids(out, ab_ref, sall_ref):
    u = out[:, :512]
    v = jnp.concatenate(
        [
            u[(2 * g + 1) * FLOC : (2 * g + 2) * FLOC] if c == 0 else -u[2 * g * FLOC : (2 * g + 1) * FLOC]
            for g in range(4)
            for c in range(2)
        ],
        axis=0,
    )
    odd = ((iota((128, 512), 1) >> 5) & 1) == 1
    real = jnp.where(odd, -v, u)
    imag = jnp.where(odd, u, v)
    for q in range(4):
        part = slice(q * 128, (q + 1) * 128)
        ab_ref[0, q] = real[:, part]
        ab_ref[1, q] = imag[:, part]
        ab_ref[2, q] = out[:, 512 + q * 128 : 512 + (q + 1) * 128]
    same = (iota((128, 128), 0) >> 5) == (iota((128, 128), 1) >> 5)
    for h in range(4):

        def gather(k):
            return jnp.concatenate(
                [
                    ab_ref[k, q, pl.ds(fl, 8, stride=FLOC), :]
                    for fl in range(4 * h, 4 * h + 4)
                    for q in range(4)
                ],
                axis=0,
            )

        b_hi, b_lo = split(jnp.where(same, gather(2), 0.0).T)
        a_hi, a_lo = split(jnp.concatenate([gather(0), gather(1)], axis=1))
        sub = (
            jnp.dot(b_hi, a_hi, preferred_element_type=F32)
            + jnp.dot(b_lo, a_hi, preferred_element_type=F32)
            + jnp.dot(b_hi, a_lo, preferred_element_type=F32)
        ) * (1.0 / FRAMES)
        sub = sub.astype(BF16)
        sall_ref[0, h * 128 : (h + 1) * 128, :] = sub[:, :128]
        sall_ref[1, h * 128 : (h + 1) * 128, :] = sub[:, 128:]


def image_chunk(start, stop, sall_ref, t0_ref, ph_ref, ct_ref):
    width = stop - start
    part = slice(start, stop)
    table = t0_ref[:, part]
    g_r = jnp.dot(sall_ref[0], table, preferred_element_type=F32).reshape(FLOC, SUB, width)
    g_i = jnp.dot(sall_ref[1], table, preferred_element_type=F32).reshape(FLOC, SUB, width)
    cos = ph_ref[0, :, part][:, None, :]
    sin = ph_ref[1, :, part][:, None, :]
    p_r = (cos * g_r - sin * g_i).astype(BF16).reshape(FLOC * SUB, width)
    p_i = (cos * g_i + sin * g_r).astype(BF16).reshape(FLOC * SUB, width)
    image = jnp.dot(ct_ref[...], jnp.concatenate([p_r, p_i], axis=0), preferred_element_type=F32)
    return image.T


def kernel(
    v_hbm, flag_hbm, taps_hbm, kr_hbm, kc_hbm, cell_hbm, out_ref,
    v_ref, flag_ref, taps_ref, kr_ref, kc_ref, cell_ref,
    xs_ref, xr_ref, t0_ref, ph_ref, ct_ref, w_ref, ab_ref, sall_ref, img_ref,
    tr_ref, zs_ref, zr_ref, ys_ref, yr_ref,
    in_sem, near, mid, far, own_sem, a_send, a_recv, t_send, t_recv, z_send, z_recv, y_send, y_recv,
):
    role = lax.axis_index("role")
    band = lax.axis_index("band")
    mt = lax.axis_index("turn")
    y_lo = (band >= NZ).astype(I32)
    mz = band - NZ * y_lo
    my = 2 * role + y_lo

    def turn_of(k):
        return {"turn": turn_at(mt, k)}

    def z_of(step):
        return {"band": y_lo * NZ + lax.rem(mz + step, NZ)}

    def y_of(step):
        y = (my + step) & (NY - 1)
        return {"role": y >> 1, "band": (y & 1) * NZ + mz}

    def tell(sem, device):
        pl.semaphore_signal(sem, inc=1, device_id=device, device_id_type=MESH)

    fetches = [
        pltpu.make_async_copy(src, dst, in_sem.at[i])
        for i, (src, dst) in enumerate(
            (
                (v_hbm, v_ref), (taps_hbm, taps_ref), (flag_hbm, flag_ref),
                (kr_hbm, kr_ref), (kc_hbm, kc_ref), (cell_hbm, cell_ref),
            )
        )
    ]
    for fetch in fetches:
        fetch.start()

    barrier = pltpu.get_barrier_semaphore()
    for k in range(NT - 1):
        tell(barrier, turn_of(k))
    for step in (1, -1):
        tell(barrier, z_of(step + NZ))
        tell(barrier, y_of(step))

    for fetch in fetches[:3]:
        fetch.wait()
    channelize(v_ref, flag_ref, taps_ref, xs_ref)

    pl.semaphore_wait(barrier, NT + 3)
    spread = []
    for k in range(NT - 1):
        dest = turn_at(mt, k)
        copy = pltpu.make_async_remote_copy(
            src_ref=xs_ref.at[dest], dst_ref=xr_ref.at[mt],
            send_sem=a_send.at[k], recv_sem=a_recv.at[mt],
            device_id=turn_of(k), device_id_type=MESH,
        )
        copy.start()
        spread.append(copy)
    own = pltpu.make_async_copy(xs_ref.at[mt], xr_ref.at[mt], own_sem)
    own.start()
    for step in (1, -1):
        tell(near, z_of(step + NZ))
        tell(near, y_of(step))

    for fetch in fetches[3:]:
        fetch.wait()
    tables(mt, my, mz, cell_ref, t0_ref, ph_ref, ct_ref)
    weights(kr_ref, kc_ref, w_ref)

    pl.semaphore_wait(near, 4)
    for step in (2, -2):
        tell(mid, z_of(step + NZ))
        tell(mid, y_of(step))

    own.wait()

    def arrived(k):
        src = turn_at(mt, k)
        pltpu.make_async_remote_copy(
            src_ref=xs_ref.at[src], dst_ref=xr_ref.at[src],
            send_sem=a_send.at[k], recv_sem=a_recv.at[src],
            device_id=turn_of(k), device_id_type=MESH,
        ).wait_recv()

    out = None
    for group in ((6,), (2, 3), (4, 5), (0, 1)):
        for k in group:
            arrived(k)
        term = stations(turn_at(mt, group[0]) >> 1, xr_ref, w_ref)
        out = term if out is None else out + term

    pl.semaphore_wait(mid, 4)
    for step in (2, -2):
        tell(far, z_of(step + NZ))

    subgrids(out, ab_ref, sall_ref)

    def turn_copy(k):
        return pltpu.make_async_remote_copy(
            src_ref=img_ref.at[pl.ds(k * PIECE, PIECE), :], dst_ref=tr_ref.at[k],
            send_sem=t_send.at[k], recv_sem=t_recv.at[k],
            device_id=turn_of(k), device_id_type=MESH,
        )

    turn_copies = []
    done = 0
    for start, stop in zip(EDGES, EDGES[1:]):
        rows = image_chunk(start, stop, sall_ref, t0_ref, ph_ref, ct_ref)
        img_ref[start:stop, :] = rows.astype(BF16)
        while done < NT - 1 and (done + 1) * PIECE <= stop:
            copy = turn_copy(done)
            copy.start()
            turn_copies.append(copy)
            done += 1
    pl.semaphore_wait(far, 2)
    total = rows[rows.shape[0] - PIECE :, :]
    for k in range(NT - 1):
        turn_copies[k].wait_recv()
        total = total + tr_ref[k].astype(F32)

    zs_ref[...] = total.astype(BF16).reshape(NZ, NY, MW)
    z_copies = []
    for k in range(NZ - 1):
        copy = pltpu.make_async_remote_copy(
            src_ref=zs_ref.at[k], dst_ref=zr_ref.at[k],
            send_sem=z_send.at[k], recv_sem=z_recv.at[k],
            device_id=z_of(ROWS_Z[k]), device_id_type=MESH,
        )
        copy.start()
        z_copies.append(copy)
    total = total[(NZ - 1) * NY :, :]
    for k in range(NZ - 1):
        z_copies[k].wait_recv()
        total = total + zr_ref[k].astype(F32)

    y_copies = []
    ys_ref[...] = total
    yr_ref[NY - 1 :, :] = total[NY - 1 :, :]
    for k in range(NY - 1):
        copy = pltpu.make_async_remote_copy(
            src_ref=ys_ref.at[pl.ds(k, 1), :], dst_ref=yr_ref.at[pl.ds(k, 1), :],
            send_sem=y_send.at[k], recv_sem=y_recv.at[k],
            device_id=y_of(ROWS_Y[k]), device_id_type=MESH,
        )
        copy.start()
        y_copies.append(copy)
    for copy in y_copies:
        copy.wait_recv()
    final = jnp.sum(yr_ref[...], axis=0, keepdims=True)
    out_ref[...] = final * SCALE
    for copy in spread + turn_copies + z_copies + y_copies:
        copy.wait_send()


def local(voltages, station_flags, filter_taps, kernel_rows, kernel_cols, cell_index):
    vmem = pl.BlockSpec(memory_space=pltpu.VMEM)
    hbm = pl.BlockSpec(memory_space=pl.ANY)
    dma = pltpu.SemaphoreType.DMA
    return pl.pallas_call(
        kernel,
        out_shape=jax.ShapeDtypeStruct((1, MW), F32),
        in_specs=[hbm] * 6,
        out_specs=vmem,
        scratch_shapes=[
            pltpu.VMEM((2 * STLOC, (FRAMES + TAPS - 1) * 2 * FINE), BF16),
            pltpu.SMEM((STLOC,), I32),
            pltpu.VMEM((TAPS * 2 * FINE, 2 * FINE), BF16),
            pltpu.VMEM((SUB, 256), BF16),
            pltpu.VMEM((SUB, 256), BF16),
            pltpu.SMEM((2, FLOC), I32),
            pltpu.VMEM((NT, 2, FLOC, 512), BF16),
            pltpu.VMEM((NT, 2, FLOC, 512), BF16),
            pltpu.VMEM((128, LW), BF16),
            pltpu.VMEM((2, FLOC, LW), F32),
            pltpu.VMEM((MW, 2 * FLOC * SUB), BF16),
            pltpu.VMEM((1024, 1024), BF16),
            pltpu.VMEM((3, 4, 128, 128), F32),
            pltpu.VMEM((2, FLOC * SUB, 128), BF16),
            pltpu.VMEM((LW, MW), BF16),
            pltpu.VMEM((NT - 1, PIECE, MW), BF16),
            pltpu.VMEM((NZ, NY, MW), BF16),
            pltpu.VMEM((NZ - 1, NY, MW), BF16),
            pltpu.VMEM((NY, MW), F32),
            pltpu.VMEM((NY, MW), F32),
            dma((6,)),
            pltpu.SemaphoreType.REGULAR,
            pltpu.SemaphoreType.REGULAR,
            pltpu.SemaphoreType.REGULAR,
            dma,
            dma((NT - 1,)),
            dma((NT,)),
            dma((NT - 1,)),
            dma((NT - 1,)),
            dma((NZ - 1,)),
            dma((NZ - 1,)),
            dma((NY - 1,)),
            dma((NY - 1,)),
        ],
        compiler_params=pltpu.CompilerParams(collective_id=0, has_side_effects=True, vmem_limit_bytes=24 << 20),
    )(
        pltpu.with_memory_space_constraint(voltages.reshape(2 * STLOC, -1), pltpu.HBM),
        pltpu.with_memory_space_constraint(station_flags, pltpu.HBM),
        pltpu.with_memory_space_constraint(filter_taps.reshape(TAPS * 2 * FINE, 2 * FINE), pltpu.HBM),
        pltpu.with_memory_space_constraint(kernel_rows.reshape(SUB, -1), pltpu.HBM),
        pltpu.with_memory_space_constraint(kernel_cols.reshape(SUB, -1), pltpu.HBM),
        pltpu.with_memory_space_constraint(cell_index.reshape(2, FLOC), pltpu.HBM),
    )


def solution(mesh):
    in_specs = (
        P(("role", "band"), None, "turn", None),
        P("turn"),
        P(),
        P(("role", "band"), None, None, None),
        P(("role", "band"), None, None, None),
        P(None, ("role", "band", "turn"), None),
    )
    out_specs = P(("role", "band", "turn"), None)
    return jax.shard_map(local, mesh=mesh, in_specs=in_specs, out_specs=out_specs, check_vma=False)
```
